32 devices in a mesh: vec: 8 (over z, y), space: 4 (over x, core).
Axes of the slice: x: 2, y: 2, z: 4, core: 2. Of those that a mesh axis runs over, the one named last changes fastest.
Arguments:
- perturbation: float32 [8, 6, 96, 512], P('vec', None, 'space'), may hold values from -40 to 40
- trajectory: bfloat16 [8, 3, 6, 96, 512], P('vec', None, None, 'space'), may hold values from -1.796875 to 1.796875
- step_order: int32 [8], replicated, may hold values from 0 to 7, each once
Outputs:
- ortho_vectors: float32 [8, 6, 96, 512], P('vec', None, 'space')
- upper_factor: float32 [8, 8], replicated
The draws below stay inside these ranges and needn't reach their ends.
Inputs may be any that keep to these rules, and one draw needn't show every extreme that they name: `step_order`: each number appears once.
All inputs are finite; a program needn't handle non-finite values.
Results may differ from the reference program's by a relative error of at most 0.0003.
Values may be sent and summed in bfloat16 or wider, within the bound.
A program may use at most 64 MiB of HBM per device.

```python
import jax
import jax.numpy as jnp
from jax import lax

NY = 512
STEPS = 2
K = 8
NX = 96
TRAJ = 8


def draw_perturbation(key, part):
    noise = jnp.clip(jax.random.normal(jax.random.fold_in(key, 11), (K, 6, NX, NY), jnp.float32), -6.0, 6.0)
    return noise


def levels(own_key, shape, split, low, top_value):
    factor_of = 1.0
    for position, blocks in split:
        heights = jax.random.uniform(jax.random.fold_in(jax.random.fold_in(own_key, 6), position), (blocks,), jnp.float32, low / len(split), top_value / len(split))
        factor_of = factor_of * jnp.repeat(jnp.exp(heights), shape[position] // blocks).reshape((-1,) + (1,) * (len(shape) - 1 - position))
    return factor_of


def gaussian(stream_key, extent, width, bound, cuts=(), dtype=jnp.bfloat16):
    array = width * jax.random.normal(stream_key, extent, jnp.float32)
    if cuts:
        array = array * levels(stream_key, extent, cuts, -0.22, 0.18)
    return jnp.clip(array, -bound, bound).astype(dtype)


def setup_inputs(seed: int = 0) -> dict:
    streams_of = jax.random.split(jax.random.key(seed), 4)
    perturbation = draw_perturbation(jax.random.fold_in(streams_of[3], 71), 0)
    trajectory = gaussian(streams_of[1], (TRAJ, 3, 6, NX, NY), 0.3, 1.796875, ((0, 8), (3, 4)))
    step_order = jax.random.permutation(streams_of[2], TRAJ).astype(jnp.int32)
    return dict(perturbation=perturbation, trajectory=trajectory, step_order=step_order)


GRAVITY_TOP = 1.0
GRAVITY_LOW = 0.5
DEPTH_TOP = 1.0
DEPTH_LOW = 1.0
CORIOLIS = 0.3
TIME_STEP = 0.25

def diff_x(field):
    return 0.5 * (field[..., 2:, :] - field[..., :-2, :])

def diff_y(field):
    return 0.5 * (jnp.roll(field, -1, -1) - jnp.roll(field, 1, -1))

def trimmed(field, amount):
    return field[..., amount:field.shape[-2] - amount, :]

def tangent(base_state, tangent_state):
    dp_top = GRAVITY_TOP * (tangent_state[..., 0, :, :] + tangent_state[..., 3, :, :])
    dp_low = dp_top + GRAVITY_LOW * tangent_state[..., 3, :, :]
    results = []
    for layer_num, (mean_depth, pressure) in enumerate(((DEPTH_TOP, dp_top), (DEPTH_LOW, dp_low))):
        offset = 3 * layer_num
        base_depth = base_state[offset] + mean_depth
        base_xvel = base_state[offset + 1]
        base_yvel = base_state[offset + 2]
        pert_depth = tangent_state[..., offset, :, :]
        pert_xvel = tangent_state[..., offset + 1, :, :]
        pert_yvel = tangent_state[..., offset + 2, :, :]
        depth_rate = -diff_x(base_depth * pert_xvel + pert_depth * base_xvel) - trimmed(diff_y(base_depth * pert_yvel + pert_depth * base_yvel), 1)
        xvel_rate = -(trimmed(base_xvel, 1) * diff_x(pert_xvel) + trimmed(pert_xvel, 1) * diff_x(base_xvel)) - trimmed(base_yvel * diff_y(pert_xvel) + pert_yvel * diff_y(base_xvel), 1) + CORIOLIS * trimmed(pert_yvel, 1) - diff_x(pressure)
        yvel_rate = -(trimmed(base_xvel, 1) * diff_x(pert_yvel) + trimmed(pert_xvel, 1) * diff_x(base_yvel)) - trimmed(base_yvel * diff_y(pert_yvel) + pert_yvel * diff_y(base_yvel), 1) - CORIOLIS * trimmed(pert_xvel, 1) - trimmed(diff_y(pressure), 1)
        results += [depth_rate, xvel_rate, yvel_rate]
    return jnp.stack(results, axis=-3)

def combine(section_num, anchor, current, change):
    if section_num == 0:
        return current + TIME_STEP * change
    if section_num == 1:
        return 0.75 * anchor + 0.25 * (current + TIME_STEP * change)
    return anchor / 3.0 + 2.0 / 3.0 * (current + TIME_STEP * change)

def pad_rows(field):
    widths = [(0, 0)] * (field.ndim - 2) + [(1, 1), (0, 0)]
    return jnp.pad(field, widths, mode='wrap')

def reference(perturbation, trajectory, step_order):
    state = perturbation
    for step_num in range(STEPS):
        sections = trajectory[step_order[step_num]].astype(jnp.float32)
        padded_sections = pad_rows(sections)

        def advance(vector):
            current = vector
            for section_num in range(3):
                change = tangent(padded_sections[section_num], pad_rows(current))
                current = combine(section_num, vector, current, change)
            return current
        state = lax.map(advance, state)
    entries = 6 * state.shape[2] * state.shape[3]
    flat_cells = state.reshape(state.shape[0], -1)
    gram_matrix = jnp.dot(flat_cells.astype(jnp.float32), flat_cells.T.astype(jnp.float32), precision=lax.Precision.HIGHEST, preferred_element_type=jnp.float32) / entries
    lower_factor = jnp.linalg.cholesky(gram_matrix)
    ortho = jax.scipy.linalg.solve_triangular(lower_factor, flat_cells, lower=True)
    return (ortho.reshape(state.shape), jnp.transpose(lower_factor))
```

```python
import functools

import jax
import jax.numpy as jnp
from jax import lax
from jax.experimental import pallas as pl
from jax.experimental.pallas import tpu as pltpu
from jax.sharding import PartitionSpec as P

STEPS = 2
SECTIONS = 3
HALO = 8

GRAVITY_TOP = 1.0
GRAVITY_LOW = 0.5
DEPTH_TOP = 1.0
DEPTH_LOW = 1.0
CORIOLIS = 0.3
TIME_STEP = 0.25

MESH = pl.DeviceIdType.MESH
F32 = jnp.float32


def remote(src, dst, send, recv, target):
    return pltpu.make_async_remote_copy(
        src_ref=src, dst_ref=dst, send_sem=send, recv_sem=recv, device_id=target, device_id_type=MESH
    )


def share_kernel(
    n, ns, order_ref, traj_ref, pert_ref,
    main_ref, lo_ref, hi_ref, plo_ref, phi_ref,
    pair, in_up, in_dn, out_up, out_dn, half, edges,
    sa, ra, su, ru, sd, rd, sc, rc, sh, rh, sp, rp,
):
    me = lax.axis_index("vec")
    tile = lax.axis_index("space")
    side = lax.rem(me, 2)
    line = me // 2
    lines = n // 2
    partner = me + 1 - 2 * side
    up_ok = line < lines - 1
    dn_ok = line > 0
    next_tile = lax.rem(tile + 1, ns)
    prev_tile = lax.rem(tile + ns - 1, ns)
    chunks = STEPS * SECTIONS
    rows = traj_ref.shape[2]

    barrier = pltpu.get_barrier_semaphore()
    pl.semaphore_signal(barrier, inc=1, device_id={"vec": partner}, device_id_type=MESH)
    pl.semaphore_signal(barrier, inc=1, device_id={"space": next_tile}, device_id_type=MESH)
    pl.semaphore_signal(barrier, inc=1, device_id={"space": prev_tile}, device_id_type=MESH)

    @pl.when(up_ok)
    def _():
        pl.semaphore_signal(barrier, inc=1, device_id={"vec": me + 2}, device_id_type=MESH)

    @pl.when(dn_ok)
    def _():
        pl.semaphore_signal(barrier, inc=1, device_id={"vec": me - 2}, device_id_type=MESH)

    pl.semaphore_wait(barrier, 3 + up_ok.astype(jnp.int32) + dn_ok.astype(jnp.int32))

    mine = pl.ds(3 * side, 3)
    other = pl.ds(3 * (1 - side), 3)

    def swap(k):
        return remote(traj_ref.at[k, other], pair.at[k], sa.at[k], ra.at[k], {"vec": partner})

    def go_up(c):
        return remote(out_up.at[c], in_up.at[c], su.at[c], ru.at[c], {"vec": me + 2})

    def go_dn(c):
        return remote(out_dn.at[c], in_dn.at[c], sd.at[c], rd.at[c], {"vec": me - 2})

    def give(c):
        return remote(half.at[c], main_ref.at[c, mine], sc.at[c], rc.at[c], {"vec": partner})

    def edge_next(c):
        return remote(edges.at[c, 1], lo_ref.at[c], sh.at[c, 1], rh.at[c, 1], {"space": next_tile})

    def edge_prev(c):
        return remote(edges.at[c, 0], hi_ref.at[c], sh.at[c, 0], rh.at[c, 0], {"space": prev_tile})

    pert_next = remote(pert_ref.at[:, pl.ds(rows - HALO, HALO)], plo_ref, sp.at[0], rp.at[0], {"space": next_tile})
    pert_prev = remote(pert_ref.at[:, pl.ds(0, HALO)], phi_ref, sp.at[1], rp.at[1], {"space": prev_tile})

    for k in range(SECTIONS):
        swap(k).start()
    pert_next.start()
    pert_prev.start()

    def owner_of(c):
        return jnp.where(c >= SECTIONS, order_ref[1], order_ref[0])

    def candidate(c):
        k = lax.rem(c, SECTIONS)
        return jnp.where(owner_of(c) == me, traj_ref[k, mine], pair[k])

    def inside(c):
        return (c >= 0) & (c < chunks)

    far = jnp.maximum(line, lines - 1 - line)

    @pl.loop(0, lines + chunks)
    def _(t):
        c_up = t - line
        c_dn = t - (lines - 1 - line)
        c_fin = t - far
        c_edge = c_fin - 1
        c_pair = t - jnp.minimum(line, lines - 1 - line)

        @pl.when((c_pair >= 0) & (c_pair < SECTIONS))
        def _():
            swap(c_pair).wait_recv()

        @pl.when(inside(c_up))
        def _():
            @pl.when(dn_ok)
            def _():
                go_up(c_up).wait_recv()

            @pl.when(up_ok)
            def _():
                here = owner_of(c_up) // 2 == line
                out_up[c_up] = jnp.where(here, candidate(c_up), in_up[c_up])
                go_up(c_up).start()

        @pl.when(inside(c_dn))
        def _():
            @pl.when(up_ok)
            def _():
                go_dn(c_dn).wait_recv()

            @pl.when(dn_ok)
            def _():
                here = owner_of(c_dn) // 2 == line
                out_dn[c_dn] = jnp.where(here, candidate(c_dn), in_dn[c_dn])
                go_dn(c_dn).start()

        @pl.when(inside(c_fin))
        def _():
            at = owner_of(c_fin) // 2
            value = jnp.where(
                at == line, candidate(c_fin), jnp.where(at < line, in_up[c_fin], in_dn[c_fin])
            )
            half[c_fin] = value
            give(c_fin).start()
            main_ref[c_fin, mine] = value

        @pl.when(inside(c_edge))
        def _():
            give(c_edge).wait_recv()
            edges[c_edge, 0] = main_ref[c_edge, :, :HALO, :]
            edges[c_edge, 1] = main_ref[c_edge, :, rows - HALO :, :]
            edge_next(c_edge).start()
            edge_prev(c_edge).start()

    @pl.loop(0, chunks)
    def _(c):
        edge_next(c).wait()
        edge_prev(c).wait()
        give(c).wait_send()

        @pl.when(up_ok)
        def _():
            go_up(c).wait_send()

        @pl.when(dn_ok)
        def _():
            go_dn(c).wait_send()

    for k in range(SECTIONS):
        swap(k).wait_send()
    pert_next.wait()
    pert_prev.wait()


def share(n, ns, order, traj, pert):
    sections, fields, rows, cols = traj.shape
    chunks = STEPS * sections
    bf = traj.dtype
    vmem = pl.BlockSpec(memory_space=pltpu.VMEM)
    piece = pltpu.VMEM((chunks, 3, rows, cols), bf)
    dma = pltpu.SemaphoreType.DMA
    return pl.pallas_call(
        functools.partial(share_kernel, n, ns),
        out_shape=(
            jax.ShapeDtypeStruct((chunks, fields, rows, cols), bf),
            jax.ShapeDtypeStruct((chunks, fields, HALO, cols), bf),
            jax.ShapeDtypeStruct((chunks, fields, HALO, cols), bf),
            jax.ShapeDtypeStruct((fields, HALO, cols), F32),
            jax.ShapeDtypeStruct((fields, HALO, cols), F32),
        ),
        in_specs=[pl.BlockSpec(memory_space=pltpu.SMEM), vmem, vmem],
        out_specs=(vmem,) * 5,
        scratch_shapes=[
            pltpu.VMEM((sections, 3, rows, cols), bf),
            piece, piece, piece, piece, piece,
            pltpu.VMEM((chunks, 2, fields, HALO, cols), bf),
            dma((sections,)), dma((sections,)),
            dma((chunks,)), dma((chunks,)),
            dma((chunks,)), dma((chunks,)),
            dma((chunks,)), dma((chunks,)),
            dma((chunks, 2)), dma((chunks, 2)),
            dma((2,)), dma((2,)),
        ],
        compiler_params=pltpu.CompilerParams(collective_id=0, has_side_effects=True),
        name="share",
    )(order, traj, pert)


def diff_x(field):
    count = field.shape[0]
    return 0.5 * (pltpu.roll(field, count - 1, 0) - pltpu.roll(field, 1, 0))


def diff_y(field):
    count = field.shape[1]
    return 0.5 * (pltpu.roll(field, count - 1, 1) - pltpu.roll(field, 1, 1))


def tangent(base, state):
    dp_top = GRAVITY_TOP * (state[0] + state[3])
    dp_low = dp_top + GRAVITY_LOW * state[3]
    rates = []
    for layer, (mean_depth, pressure) in enumerate(((DEPTH_TOP, dp_top), (DEPTH_LOW, dp_low))):
        at = 3 * layer
        depth = base[at] + mean_depth
        u, v = base[at + 1], base[at + 2]
        dh, du, dv = state[at], state[at + 1], state[at + 2]
        rates.append(-diff_x(depth * du + dh * u) - diff_y(depth * dv + dh * v))
        rates.append(
            -(u * diff_x(du) + du * diff_x(u)) - (v * diff_y(du) + dv * diff_y(u))
            + CORIOLIS * dv - diff_x(pressure)
        )
        rates.append(
            -(u * diff_x(dv) + du * diff_x(v)) - (v * diff_y(dv) + dv * diff_y(v))
            - CORIOLIS * du - diff_y(pressure)
        )
    return rates


def combine(section, anchor, current, change):
    if section == 0:
        return current + TIME_STEP * change
    if section == 1:
        return 0.75 * anchor + 0.25 * (current + TIME_STEP * change)
    return anchor / 3.0 + 2.0 / 3.0 * (current + TIME_STEP * change)


def steps_kernel(per, main_ref, lo_ref, hi_ref, pert_ref, plo_ref, phi_ref, out_ref, anchor, work):
    fields, rows, cols = pert_ref.shape
    anchor[:, :HALO] = plo_ref[...]
    anchor[:, HALO : HALO + rows] = pert_ref[...]
    anchor[:, HALO + rows :] = phi_ref[...]
    work[...] = anchor[...]
    for c in range(STEPS * SECTIONS):
        base = [
            jnp.concatenate(
                [lo_ref[c, f].astype(F32), main_ref[c, f].astype(F32), hi_ref[c, f].astype(F32)], axis=0
            )
            for f in range(fields)
        ]
        current = [work[f] for f in range(fields)]
        change = tangent(base, current)
        section = c % SECTIONS
        for f in range(fields):
            value = combine(section, anchor[f], current[f], change[f])
            work[f] = value
            if section == SECTIONS - 1:
                anchor[f] = value
    units = tiles_of(fields, rows, cols)
    for number, (f, r, l) in enumerate(units):
        out_ref[number // per, pl.ds((number % per) * 8, 8), :] = work[
            f, HALO + r : HALO + r + 8, l : l + 128
        ]
    for number in range(len(units), out_ref.shape[0] * per):
        out_ref[number // per, pl.ds((number % per) * 8, 8), :] = jnp.zeros((8, 128), F32)


def tiles_of(fields, rows, cols):
    return [
        (f, r, l) for f in range(fields) for r in range(0, rows, 8) for l in range(0, cols, 128)
    ]


def run_steps(n, per, main, lo, hi, pert, plo, phi):
    fields, rows, cols = pert.shape
    vmem = pl.BlockSpec(memory_space=pltpu.VMEM)
    full = pltpu.VMEM((fields, rows + 2 * HALO, cols), F32)
    return pl.pallas_call(
        functools.partial(steps_kernel, per),
        out_shape=jax.ShapeDtypeStruct((n, per * 8, 128), F32),
        in_specs=[vmem] * 6,
        out_specs=vmem,
        scratch_shapes=[full, full],
        name="steps",
    )(main, lo, hi, pert, plo, phi)


def ortho_kernel(
    n, ns, per, entries, x_ref, out_ref, upper_ref,
    cols_ref, back, result, gspace, gvec, mine_s, mine_v,
    s1, r1, s2, r2, s3, r3, s4, r4,
):
    me = lax.axis_index("vec")
    tile = lax.axis_index("space")
    barrier = pltpu.get_barrier_semaphore()
    for d in range(1, n):
        pl.semaphore_signal(barrier, inc=1, device_id={"vec": lax.rem(me + d, n)}, device_id_type=MESH)
    for d in range(1, ns):
        pl.semaphore_signal(barrier, inc=1, device_id={"space": lax.rem(tile + d, ns)}, device_id_type=MESH)
    pl.semaphore_wait(barrier, n + ns - 2)

    def peers(count, here, axis, src, dst, send, recv):
        made = []
        for d in range(1, count):
            to = lax.rem(here + d, count)
            made.append(remote(src(to), dst, send.at[d], recv.at[d], {axis: to}))
        return made

    first = peers(n, me, "vec", lambda to: x_ref.at[to], cols_ref.at[me], s1, r1)
    for copy in first:
        copy.start()
    cols_ref[me] = x_ref[me]
    for copy in first:
        copy.wait_recv()

    lanes = lax.broadcasted_iota(jnp.int32, (n, 128), 1)
    rows = lax.broadcasted_iota(jnp.int32, (n, 128), 0)
    gram = jnp.zeros((n, 128), F32)
    for i in range(n):
        line = jnp.sum(cols_ref[...] * cols_ref[i][None], axis=1)
        gram = gram + jnp.where(lanes == i, jnp.sum(line, axis=1, keepdims=True), 0.0)

    mine_s[...] = gram
    second = peers(ns, tile, "space", lambda to: mine_s, gspace.at[tile], s2, r2)
    for copy in second:
        copy.start()
    gspace[tile] = gram
    for copy in second:
        copy.wait_recv()
    gram = gspace[0]
    for i in range(1, ns):
        gram = gram + gspace[i]

    mine_v[...] = gram
    third = peers(n, me, "vec", lambda to: mine_v, gvec.at[me], s3, r3)
    for copy in third:
        copy.start()
    gvec[me] = gram
    for copy in third:
        copy.wait_recv()
    gram = gvec[0]
    for i in range(1, n):
        gram = gram + gvec[i]

    a = jnp.where(lanes < n, gram / entries, 0.0) + jnp.where(lanes == rows + n, 1.0, 0.0)
    for k in range(n):
        pivot_row = a[k : k + 1, :]
        column = jnp.sum(jnp.where(lanes == k, a, 0.0), axis=1, keepdims=True)
        factor = jnp.where(rows[:, :1] > k, column / column[k : k + 1, :], 0.0)
        a = a - factor * pivot_row
    diagonal = jnp.sum(jnp.where(lanes == rows, a, 0.0), axis=1, keepdims=True)
    a = a / jnp.sqrt(diagonal)
    upper_ref[...] = jnp.where(lanes >= rows, a, 0.0)

    for i in range(n):
        total = jnp.broadcast_to(a[i : i + 1, n : n + 1], cols_ref.shape[1:]) * cols_ref[0]
        for j in range(1, i + 1):
            total = total + jnp.broadcast_to(a[i : i + 1, n + j : n + j + 1], cols_ref.shape[1:]) * cols_ref[j]
        result[i] = total

    fourth = peers(n, me, "vec", lambda to: result.at[to], back.at[me], s4, r4)
    for copy in fourth:
        copy.start()
    back[me] = result[me]
    for copy in fourth:
        copy.wait_recv()
    fields, height, width = out_ref.shape
    for number, (f, r, l) in enumerate(tiles_of(fields, height, width)):
        out_ref[f, r : r + 8, l : l + 128] = back[number // per, pl.ds((number % per) * 8, 8), :]
    for copy in first + second + third + fourth:
        copy.wait_send()


def orthonormalize(n, ns, per, shape, x):
    vmem = pl.BlockSpec(memory_space=pltpu.VMEM)
    dma = pltpu.SemaphoreType.DMA
    fields, rows, cols = shape
    return pl.pallas_call(
        functools.partial(ortho_kernel, n, ns, per, float(fields * rows * cols * ns)),
        out_shape=(jax.ShapeDtypeStruct(shape, F32), jax.ShapeDtypeStruct((n, 128), F32)),
        in_specs=[vmem],
        out_specs=(vmem, vmem),
        scratch_shapes=[
            pltpu.VMEM(x.shape, F32), pltpu.VMEM(x.shape, F32), pltpu.VMEM(x.shape, F32),
            pltpu.VMEM((ns, n, 128), F32), pltpu.VMEM((n, n, 128), F32),
            pltpu.VMEM((n, 128), F32), pltpu.VMEM((n, 128), F32),
            dma((n,)), dma((n,)), dma((ns,)), dma((ns,)),
            dma((n,)), dma((n,)), dma((n,)), dma((n,)),
        ],
        compiler_params=pltpu.CompilerParams(collective_id=1, has_side_effects=True),
        name="ortho",
    )(x)


def body(n, ns, perturbation, trajectory, step_order):
    pert, traj = perturbation[0], trajectory[0]
    fields, rows, cols = pert.shape
    per = -(-(fields * (rows // 8) * (cols // 128)) // n)
    main, lo, hi, plo, phi = share(n, ns, step_order, traj, pert)
    x = run_steps(n, per, main, lo, hi, pert, plo, phi)
    out, upper = orthonormalize(n, ns, per, pert.shape, x)
    return out[None], upper[:, :n]


def solution(mesh):
    n, ns = mesh.shape["vec"], mesh.shape["space"]
    in_specs = (P("vec", None, "space", None), P("vec", None, None, "space", None), P())
    out_specs = (P("vec", None, "space", None), P())
    return jax.shard_map(
        functools.partial(body, n, ns), mesh=mesh, in_specs=in_specs, out_specs=out_specs, check_vma=False
    )
```

```python
import functools

import jax
import jax.numpy as jnp
from jax import lax
from jax.experimental import pallas as pl
from jax.experimental.pallas import tpu as pltpu
from jax.sharding import PartitionSpec as P

STEPS = 2
SECTIONS = 3
LAG = 3
HALO = 8

GRAVITY_TOP = 1.0
GRAVITY_LOW = 0.5
DEPTH_TOP = 1.0
DEPTH_LOW = 1.0
CORIOLIS = 0.3
TIME_STEP = 0.25

MESH = pl.DeviceIdType.MESH
F32 = jnp.float32


def remote(src, dst, send, recv, target):
    return pltpu.make_async_remote_copy(
        src_ref=src, dst_ref=dst, send_sem=send, recv_sem=recv, device_id=target, device_id_type=MESH
    )


def diff_x(field):
    count = field.shape[0]
    return 0.5 * (pltpu.roll(field, count - 1, 0) - pltpu.roll(field, 1, 0))


def diff_y(field):
    count = field.shape[1]
    return 0.5 * (pltpu.roll(field, count - 1, 1) - pltpu.roll(field, 1, 1))


def tangent(base, state):
    dp_top = GRAVITY_TOP * (state[0] + state[3])
    dp_low = dp_top + GRAVITY_LOW * state[3]
    rates = []
    for layer, (mean_depth, pressure) in enumerate(((DEPTH_TOP, dp_top), (DEPTH_LOW, dp_low))):
        at = 3 * layer
        depth = base[at] + mean_depth
        u, v = base[at + 1], base[at + 2]
        dh, du, dv = state[at], state[at + 1], state[at + 2]
        rates.append(-diff_x(depth * du + dh * u) - diff_y(depth * dv + dh * v))
        rates.append(
            -(u * diff_x(du) + du * diff_x(u)) - (v * diff_y(du) + dv * diff_y(u))
            + CORIOLIS * dv - diff_x(pressure)
        )
        rates.append(
            -(u * diff_x(dv) + du * diff_x(v)) - (v * diff_y(dv) + dv * diff_y(v))
            - CORIOLIS * du - diff_y(pressure)
        )
    return rates


def tiles_of(fields, rows, cols):
    return [
        (f, r, l) for f in range(fields) for r in range(0, rows, 8) for l in range(0, cols, 128)
    ]


def whole_kernel(
    n, ns, per, entries, order_ref, traj_ref, pert_ref,
    back, upper_ref,
    main, lo, hi, plo, phi, pair, in_up, in_dn, out_up, out_dn, edges, anchor, work,
    x_ref, cols_ref, result, gspace, gvec, mine_s, mine_v,
    sa, ra, su, ru, sd, rd, sc, rc, sh, rh, sp, rp,
    s1, r1, s2, r2, s3, r3, s4, r4,
):
    me = lax.axis_index("vec")
    tile = lax.axis_index("space")
    side = lax.rem(me, 2)
    line = me // 2
    lines = n // 2
    partner = me + 1 - 2 * side
    up_ok = line < lines - 1
    dn_ok = line > 0
    next_tile = lax.rem(tile + 1, ns)
    prev_tile = lax.rem(tile + ns - 1, ns)
    fields, rows, cols = pert_ref.shape
    chunks = STEPS * SECTIONS * 3
    parts = SECTIONS * 3

    barrier = pltpu.get_barrier_semaphore()
    for d in range(1, n):
        pl.semaphore_signal(barrier, inc=1, device_id={"vec": lax.rem(me + d, n)}, device_id_type=MESH)
    for d in range(1, ns):
        pl.semaphore_signal(barrier, inc=1, device_id={"space": lax.rem(tile + d, ns)}, device_id_type=MESH)
    pl.semaphore_wait(barrier, n + ns - 2)

    def swap(p):
        k, f = lax.div(p, 3), lax.rem(p, 3)
        return remote(
            traj_ref.at[k, 3 * (1 - side) + f], pair.at[p], sa.at[p], ra.at[p], {"vec": partner}
        )

    def go_up(c):
        return remote(out_up.at[c], in_up.at[c], su.at[c], ru.at[c], {"vec": me + 2})

    def go_dn(c):
        return remote(out_dn.at[c], in_dn.at[c], sd.at[c], rd.at[c], {"vec": me - 2})

    def give(c):
        place = main.at[lax.div(c, 3), 3 * side + lax.rem(c, 3)]
        return remote(place, place, sc.at[c], rc.at[c], {"vec": partner})

    def edge_next(c):
        return remote(edges.at[c, 1], lo.at[c], sh.at[c, 1], rh.at[c, 1], {"space": next_tile})

    def edge_prev(c):
        return remote(edges.at[c, 0], hi.at[c], sh.at[c, 0], rh.at[c, 0], {"space": prev_tile})

    pert_next = remote(pert_ref.at[:, pl.ds(rows - HALO, HALO)], plo, sp.at[0], rp.at[0], {"space": next_tile})
    pert_prev = remote(pert_ref.at[:, pl.ds(0, HALO)], phi, sp.at[1], rp.at[1], {"space": prev_tile})

    @pl.loop(0, parts)
    def _(p):
        swap(p).start()

    pert_next.start()
    pert_prev.start()

    def owner_of(c):
        return jnp.where(c >= parts, order_ref[1], order_ref[0])

    def candidate(c):
        p = lax.rem(c, parts)
        own = traj_ref[lax.div(p, 3), 3 * side + lax.rem(p, 3)]
        return jnp.where(owner_of(c) == me, own, pair[p])

    def inside(c):
        return (c >= 0) & (c < chunks)

    near = LAG * jnp.minimum(line, lines - 1 - line)
    far = LAG * jnp.maximum(line, lines - 1 - line)
    anchor[:, HALO : HALO + rows] = pert_ref[...]

    @pl.loop(0, LAG * (lines - 1) + chunks + 2 * LAG)
    def _(t):
        c_pair = t - near
        c_up = t - LAG * line
        c_dn = t - LAG * (lines - 1 - line)
        c_fin = t - far
        c_edge = c_fin - LAG
        c_run = c_edge - LAG

        @pl.when((c_pair >= 0) & (c_pair < parts))
        def _():
            swap(c_pair).wait_recv()

        @pl.when(inside(c_up))
        def _():
            @pl.when(dn_ok)
            def _():
                go_up(c_up).wait_recv()

            @pl.when(up_ok)
            def _():
                here = lax.div(owner_of(c_up), 2) == line
                out_up[c_up] = jnp.where(here, candidate(c_up), in_up[c_up])
                go_up(c_up).start()

        @pl.when(inside(c_dn))
        def _():
            @pl.when(up_ok)
            def _():
                go_dn(c_dn).wait_recv()

            @pl.when(dn_ok)
            def _():
                here = lax.div(owner_of(c_dn), 2) == line
                out_dn[c_dn] = jnp.where(here, candidate(c_dn), in_dn[c_dn])
                go_dn(c_dn).start()

        @pl.when(inside(c_fin))
        def _():
            at = lax.div(owner_of(c_fin), 2)
            main[lax.div(c_fin, 3), 3 * side + lax.rem(c_fin, 3)] = jnp.where(
                at == line, candidate(c_fin), jnp.where(at < line, in_up[c_fin], in_dn[c_fin])
            )
            give(c_fin).start()

        @pl.when(inside(c_edge))
        def _():
            give(c_edge).wait_recv()
            section, f = lax.div(c_edge, 3), lax.rem(c_edge, 3)
            for layer in range(2):
                edges[c_edge, 0, layer] = main[section, 3 * layer + f, :HALO, :]
                edges[c_edge, 1, layer] = main[section, 3 * layer + f, rows - HALO :, :]
            edge_next(c_edge).start()
            edge_prev(c_edge).start()

        @pl.when(c_run == 0)
        def _():
            pert_next.wait()
            pert_prev.wait()
            anchor[:, :HALO] = plo[...]
            anchor[:, HALO + rows :] = phi[...]
            work[...] = anchor[...]

        @pl.when(inside(c_run))
        def _():
            edge_next(c_run).wait()
            edge_prev(c_run).wait()

        @pl.when(inside(c_run) & (lax.rem(c_run, 3) == 2))
        def _():
            number = lax.div(c_run, 3)
            section = lax.rem(number, SECTIONS)
            base = [
                jnp.concatenate(
                    [
                        lo[3 * number + f % 3, f // 3].astype(F32),
                        main[number, f].astype(F32),
                        hi[3 * number + f % 3, f // 3].astype(F32),
                    ],
                    axis=0,
                )
                for f in range(fields)
            ]
            current = [work[f] for f in range(fields)]
            change = tangent(base, current)
            keep = jnp.where(section == 0, 0.0, jnp.where(section == 1, 0.75, 1.0 / 3.0)).astype(F32)
            take = jnp.where(section == 0, 1.0, jnp.where(section == 1, 0.25, 2.0 / 3.0)).astype(F32)
            for f in range(fields):
                work[f] = keep * anchor[f] + take * (current[f] + TIME_STEP * change[f])

            @pl.when(section == SECTIONS - 1)
            def _():
                anchor[...] = work[...]

    units = tiles_of(fields, rows, cols)
    for number, (f, r, l) in enumerate(units):
        x_ref[number // per, pl.ds((number % per) * 8, 8), :] = work[
            f, HALO + r : HALO + r + 8, l : l + 128
        ]
    for number in range(len(units), n * per):
        x_ref[number // per, pl.ds((number % per) * 8, 8), :] = jnp.zeros((8, 128), F32)

    def peers(count, here, axis, src, dst, send, recv):
        made = []
        for d in range(1, count):
            to = lax.rem(here + d, count)
            made.append(remote(src(to), dst, send.at[d], recv.at[d], {axis: to}))
        return made

    first = peers(n, me, "vec", lambda to: x_ref.at[to], cols_ref.at[me], s1, r1)
    for copy in first:
        copy.start()
    cols_ref[me] = x_ref[me]

    @pl.loop(0, parts)
    def _(p):
        swap(p).wait_send()

    @pl.loop(0, chunks)
    def _(c):
        give(c).wait_send()

        @pl.when(up_ok)
        def _():
            go_up(c).wait_send()

        @pl.when(dn_ok)
        def _():
            go_dn(c).wait_send()

    for copy in first:
        copy.wait_recv()

    lanes = lax.broadcasted_iota(jnp.int32, (n, 128), 1)
    rows = lax.broadcasted_iota(jnp.int32, (n, 128), 0)
    gram = jnp.zeros((n, 128), F32)
    for i in range(n):
        line = jnp.sum(cols_ref[...] * cols_ref[i][None], axis=1)
        gram = gram + jnp.where(lanes == i, jnp.sum(line, axis=1, keepdims=True), 0.0)

    mine_s[...] = gram
    second = peers(ns, tile, "space", lambda to: mine_s, gspace.at[tile], s2, r2)
    for copy in second:
        copy.start()
    gspace[tile] = gram
    for copy in second:
        copy.wait_recv()
    gram = gspace[0]
    for i in range(1, ns):
        gram = gram + gspace[i]

    mine_v[...] = gram
    third = peers(n, me, "vec", lambda to: mine_v, gvec.at[me], s3, r3)
    for copy in third:
        copy.start()
    gvec[me] = gram
    for copy in third:
        copy.wait_recv()
    gram = gvec[0]
    for i in range(1, n):
        gram = gram + gvec[i]

    a = jnp.where(lanes < n, gram / entries, 0.0) + jnp.where(lanes == rows + n, 1.0, 0.0)
    for k in range(n):
        pivot_row = a[k : k + 1, :]
        column = jnp.sum(jnp.where(lanes == k, a, 0.0), axis=1, keepdims=True)
        factor = jnp.where(rows[:, :1] > k, column / column[k : k + 1, :], 0.0)
        a = a - factor * pivot_row
    diagonal = jnp.sum(jnp.where(lanes == rows, a, 0.0), axis=1, keepdims=True)
    a = a / jnp.sqrt(diagonal)
    upper_ref[...] = jnp.where(lanes >= rows, a, 0.0)

    for i in range(n):
        total = jnp.broadcast_to(a[i : i + 1, n : n + 1], cols_ref.shape[1:]) * cols_ref[0]
        for j in range(1, i + 1):
            total = total + jnp.broadcast_to(a[i : i + 1, n + j : n + j + 1], cols_ref.shape[1:]) * cols_ref[j]
        result[i] = total

    fourth = peers(n, me, "vec", lambda to: result.at[to], back.at[me], s4, r4)
    for copy in fourth:
        copy.start()
    back[me] = result[me]
    for copy in fourth:
        copy.wait_recv()
    for copy in first + second + third + fourth:
        copy.wait_send()


def body(n, ns, perturbation, trajectory, step_order):
    pert, traj = perturbation[0], trajectory[0]
    fields, rows, cols = pert.shape
    count = fields * (rows // 8) * (cols // 128)
    per = -(-count // n)
    sections = traj.shape[0]
    chunks, bf = STEPS * sections * 3, traj.dtype
    vmem = pl.BlockSpec(memory_space=pltpu.VMEM)
    piece = pltpu.VMEM((chunks, rows, cols), bf)
    rim = pltpu.VMEM((chunks, 2, HALO, cols), bf)
    fringe = pltpu.VMEM((fields, HALO, cols), F32)
    full = pltpu.VMEM((fields, rows + 2 * HALO, cols), F32)
    slices = pltpu.VMEM((n, per * 8, 128), F32)
    small = pltpu.VMEM((n, 128), F32)
    dma = pltpu.SemaphoreType.DMA
    back, upper = pl.pallas_call(
        functools.partial(whole_kernel, n, ns, per, float(fields * rows * cols * ns)),
        out_shape=(
            jax.ShapeDtypeStruct((n, per * 8, 128), F32),
            jax.ShapeDtypeStruct((n, 128), F32),
        ),
        in_specs=[pl.BlockSpec(memory_space=pltpu.SMEM), vmem, vmem],
        out_specs=(vmem, vmem),
        scratch_shapes=[
            pltpu.VMEM((STEPS * sections, fields, rows, cols), bf),
            rim, rim, fringe, fringe,
            pltpu.VMEM((sections * 3, rows, cols), bf),
            piece, piece, piece, piece,
            pltpu.VMEM((chunks, 2, 2, HALO, cols), bf),
            full, full,
            slices, slices, slices,
            pltpu.VMEM((ns, n, 128), F32), pltpu.VMEM((n, n, 128), F32), small, small,
            dma((sections * 3,)), dma((sections * 3,)),
            dma((chunks,)), dma((chunks,)),
            dma((chunks,)), dma((chunks,)),
            dma((chunks,)), dma((chunks,)),
            dma((chunks, 2)), dma((chunks, 2)),
            dma((2,)), dma((2,)),
            dma((n,)), dma((n,)), dma((ns,)), dma((ns,)),
            dma((n,)), dma((n,)), dma((n,)), dma((n,)),
        ],
        compiler_params=pltpu.CompilerParams(collective_id=0, has_side_effects=True),
        name="whole",
    )(step_order, traj, pert)
    out = back.reshape(n * per, 8, 128)[:count].reshape(fields, rows // 8, cols // 128, 8, 128)
    out = out.transpose(0, 1, 3, 2, 4).reshape(pert.shape)
    return out[None], upper[:, :n]


def solution(mesh):
    n, ns = mesh.shape["vec"], mesh.shape["space"]
    in_specs = (P("vec", None, "space", None), P("vec", None, None, "space", None), P())
    out_specs = (P("vec", None, "space", None), P())
    return jax.shard_map(
        functools.partial(body, n, ns), mesh=mesh, in_specs=in_specs, out_specs=out_specs, check_vma=False
    )
```

```python
import functools

import jax
import jax.numpy as jnp
from jax import lax
from jax.experimental import pallas as pl
from jax.experimental.pallas import tpu as pltpu
from jax.sharding import PartitionSpec as P

STEPS = 2
SECTIONS = 3
RIM_LAG = 7
LAG = 6
HALO = 8

GRAVITY_TOP = 1.0
GRAVITY_LOW = 0.5
DEPTH_TOP = 1.0
DEPTH_LOW = 1.0
CORIOLIS = 0.3
TIME_STEP = 0.25

MESH = pl.DeviceIdType.MESH
F32 = jnp.float32


def remote(src, dst, send, recv, target):
    return pltpu.make_async_remote_copy(
        src_ref=src, dst_ref=dst, send_sem=send, recv_sem=recv, device_id=target, device_id_type=MESH
    )


def diff_x(field):
    count = field.shape[0]
    return 0.5 * (pltpu.roll(field, count - 1, 0) - pltpu.roll(field, 1, 0))


def diff_y(field):
    count = field.shape[1]
    return 0.5 * (pltpu.roll(field, count - 1, 1) - pltpu.roll(field, 1, 1))


def tangent(base, state):
    dp_top = GRAVITY_TOP * (state[0] + state[3])
    dp_low = dp_top + GRAVITY_LOW * state[3]
    rates = []
    for layer, (mean_depth, pressure) in enumerate(((DEPTH_TOP, dp_top), (DEPTH_LOW, dp_low))):
        at = 3 * layer
        depth = base[at] + mean_depth
        u, v = base[at + 1], base[at + 2]
        dh, du, dv = state[at], state[at + 1], state[at + 2]
        rates.append(-diff_x(depth * du + dh * u) - diff_y(depth * dv + dh * v))
        rates.append(
            -(u * diff_x(du) + du * diff_x(u)) - (v * diff_y(du) + dv * diff_y(u))
            + CORIOLIS * dv - diff_x(pressure)
        )
        rates.append(
            -(u * diff_x(dv) + du * diff_x(v)) - (v * diff_y(dv) + dv * diff_y(v))
            - CORIOLIS * du - diff_y(pressure)
        )
    return rates


def tiles_of(fields, rows, cols):
    return [
        (f, r, l) for f in range(fields) for r in range(0, rows, 8) for l in range(0, cols, 128)
    ]


def whole_kernel(
    n, ns, per, entries, order_ref, traj_ref, pert_ref,
    back, upper_ref,
    main, lo, hi, plo, phi, pair, in_up, in_dn, out_up, out_dn, edges, anchor, work,
    x_ref, cols_ref, result, gspace, gvec, mine_s, mine_v,
    sa, ra, su, ru, sd, rd, sc, rc, sh, rh, sp, rp,
    s1, r1, s2, r2, s3, r3, s4, r4,
):
    me = lax.axis_index("vec")
    tile = lax.axis_index("space")
    side = lax.rem(me, 2)
    line = me // 2
    lines = n // 2
    partner = me + 1 - 2 * side
    up_ok = line < lines - 1
    dn_ok = line > 0
    next_tile = lax.rem(tile + 1, ns)
    prev_tile = lax.rem(tile + ns - 1, ns)
    fields, rows, cols = pert_ref.shape
    chunks = STEPS * SECTIONS * 3
    parts = SECTIONS * 3

    barrier = pltpu.get_barrier_semaphore()
    pl.semaphore_signal(barrier, inc=1, device_id={"vec": partner}, device_id_type=MESH)
    pl.semaphore_signal(barrier, inc=1, device_id={"space": next_tile}, device_id_type=MESH)
    pl.semaphore_signal(barrier, inc=1, device_id={"space": prev_tile}, device_id_type=MESH)

    @pl.when(up_ok)
    def _():
        pl.semaphore_signal(barrier, inc=1, device_id={"vec": me + 2}, device_id_type=MESH)

    @pl.when(dn_ok)
    def _():
        pl.semaphore_signal(barrier, inc=1, device_id={"vec": me - 2}, device_id_type=MESH)

    pl.semaphore_wait(barrier, 3 + up_ok.astype(jnp.int32) + dn_ok.astype(jnp.int32))

    def swap(p):
        k, f = lax.div(p, 3), lax.rem(p, 3)
        return remote(
            traj_ref.at[k, 3 * (1 - side) + f], pair.at[p], sa.at[p], ra.at[p], {"vec": partner}
        )

    def go_up(c):
        return remote(out_up.at[c], in_up.at[c], su.at[c], ru.at[c], {"vec": me + 2})

    def go_dn(c):
        return remote(out_dn.at[c], in_dn.at[c], sd.at[c], rd.at[c], {"vec": me - 2})

    def give(c):
        place = main.at[lax.div(c, 3), 3 * side + lax.rem(c, 3)]
        return remote(place, place, sc.at[c], rc.at[c], {"vec": partner})

    def edge_next(c):
        return remote(edges.at[c, 1], lo.at[c], sh.at[c, 1], rh.at[c, 1], {"space": next_tile})

    def edge_prev(c):
        return remote(edges.at[c, 0], hi.at[c], sh.at[c, 0], rh.at[c, 0], {"space": prev_tile})

    pert_next = remote(pert_ref.at[:, pl.ds(rows - HALO, HALO)], plo, sp.at[0], rp.at[0], {"space": next_tile})
    pert_prev = remote(pert_ref.at[:, pl.ds(0, HALO)], phi, sp.at[1], rp.at[1], {"space": prev_tile})

    @pl.loop(0, parts)
    def _(p):
        swap(p).start()

    pert_next.start()
    pert_prev.start()

    def owner_of(c):
        return jnp.where(c >= parts, order_ref[1], order_ref[0])

    def candidate(c):
        p = lax.rem(c, parts)
        own = traj_ref[lax.div(p, 3), 3 * side + lax.rem(p, 3)]
        return jnp.where(owner_of(c) == me, own, pair[p])

    def inside(c):
        return (c >= 0) & (c < chunks)

    near = LAG * jnp.minimum(line, lines - 1 - line)
    far = LAG * jnp.maximum(line, lines - 1 - line)
    anchor[:, HALO : HALO + rows] = pert_ref[...]

    @pl.loop(0, LAG * (lines - 1) + chunks + LAG + RIM_LAG)
    def _(t):
        c_pair = t - near
        c_up = t - LAG * line
        c_dn = t - LAG * (lines - 1 - line)
        c_fin = t - far
        c_edge = c_fin - LAG
        c_run = c_edge - RIM_LAG

        @pl.when((c_pair >= 0) & (c_pair < parts))
        def _():
            swap(c_pair).wait_recv()

        @pl.when(inside(c_up))
        def _():
            @pl.when(dn_ok)
            def _():
                go_up(c_up).wait_recv()

            @pl.when(up_ok)
            def _():
                here = lax.div(owner_of(c_up), 2) == line
                out_up[c_up] = jnp.where(here, candidate(c_up), in_up[c_up])
                go_up(c_up).start()

        @pl.when(inside(c_dn))
        def _():
            @pl.when(up_ok)
            def _():
                go_dn(c_dn).wait_recv()

            @pl.when(dn_ok)
            def _():
                here = lax.div(owner_of(c_dn), 2) == line
                out_dn[c_dn] = jnp.where(here, candidate(c_dn), in_dn[c_dn])
                go_dn(c_dn).start()

        @pl.when(inside(c_fin))
        def _():
            at = lax.div(owner_of(c_fin), 2)
            main[lax.div(c_fin, 3), 3 * side + lax.rem(c_fin, 3)] = jnp.where(
                at == line, candidate(c_fin), jnp.where(at < line, in_up[c_fin], in_dn[c_fin])
            )
            give(c_fin).start()

        @pl.when(inside(c_edge))
        def _():
            give(c_edge).wait_recv()

        @pl.when(inside(c_edge) & (lax.rem(c_edge, 3) == 2))
        def _():
            section = lax.div(c_edge, 3)
            edges[section, 0] = main[section, :, :HALO, :]
            edges[section, 1] = main[section, :, rows - HALO :, :]
            edge_next(section).start()
            edge_prev(section).start()

        @pl.when(c_run == 0)
        def _():
            pert_next.wait()
            pert_prev.wait()
            anchor[:, :HALO] = plo[...]
            anchor[:, HALO + rows :] = phi[...]
            work[...] = anchor[...]

        @pl.when(inside(c_run) & (lax.rem(c_run, 3) == 2))
        def _():
            number = lax.div(c_run, 3)
            section = lax.rem(number, SECTIONS)
            edge_next(number).wait()
            edge_prev(number).wait()
            base = [
                jnp.concatenate(
                    [
                        lo[number, f].astype(F32),
                        main[number, f].astype(F32),
                        hi[number, f].astype(F32),
                    ],
                    axis=0,
                )
                for f in range(fields)
            ]
            current = [work[f] for f in range(fields)]
            change = tangent(base, current)
            keep = jnp.where(section == 0, 0.0, jnp.where(section == 1, 0.75, 1.0 / 3.0)).astype(F32)
            take = jnp.where(section == 0, 1.0, jnp.where(section == 1, 0.25, 2.0 / 3.0)).astype(F32)
            for f in range(fields):
                work[f] = keep * anchor[f] + take * (current[f] + TIME_STEP * change[f])

            @pl.when(section == SECTIONS - 1)
            def _():
                anchor[...] = work[...]

    units = tiles_of(fields, rows, cols)
    for number, (f, r, l) in enumerate(units):
        x_ref[number // per, pl.ds((number % per) * 8, 8), :] = work[
            f, HALO + r : HALO + r + 8, l : l + 128
        ]
    for number in range(len(units), n * per):
        x_ref[number // per, pl.ds((number % per) * 8, 8), :] = jnp.zeros((8, 128), F32)

    def peers(count, here, axis, src, dst, send, recv):
        made = []
        for d in range(1, count):
            to = lax.rem(here + d, count)
            made.append(remote(src(to), dst, send.at[d], recv.at[d], {axis: to}))
        return made

    first = peers(n, me, "vec", lambda to: x_ref.at[to], cols_ref.at[me], s1, r1)
    for copy in first:
        copy.start()
    cols_ref[me] = x_ref[me]

    @pl.loop(0, parts)
    def _(p):
        swap(p).wait_send()

    @pl.loop(0, chunks)
    def _(c):
        give(c).wait_send()

        @pl.when(up_ok)
        def _():
            go_up(c).wait_send()

        @pl.when(dn_ok)
        def _():
            go_dn(c).wait_send()

    for copy in first:
        copy.wait_recv()

    lanes = lax.broadcasted_iota(jnp.int32, (n, 128), 1)
    rows = lax.broadcasted_iota(jnp.int32, (n, 128), 0)
    gram = jnp.zeros((n, 128), F32)
    for i in range(n):
        line = jnp.sum(cols_ref[...] * cols_ref[i][None], axis=1)
        gram = gram + jnp.where(lanes == i, jnp.sum(line, axis=1, keepdims=True), 0.0)

    mine_s[...] = gram
    second = peers(ns, tile, "space", lambda to: mine_s, gspace.at[tile], s2, r2)
    for copy in second:
        copy.start()
    gspace[tile] = gram
    for copy in second:
        copy.wait_recv()
    gram = gspace[0]
    for i in range(1, ns):
        gram = gram + gspace[i]

    mine_v[...] = gram
    third = peers(n, me, "vec", lambda to: mine_v, gvec.at[me], s3, r3)
    for copy in third:
        copy.start()
    gvec[me] = gram
    for copy in third:
        copy.wait_recv()
    gram = gvec[0]
    for i in range(1, n):
        gram = gram + gvec[i]

    a = jnp.where(lanes < n, gram / entries, 0.0) + jnp.where(lanes == rows + n, 1.0, 0.0)
    for k in range(n):
        pivot_row = a[k : k + 1, :]
        column = jnp.sum(jnp.where(lanes == k, a, 0.0), axis=1, keepdims=True)
        factor = jnp.where(rows[:, :1] > k, column / column[k : k + 1, :], 0.0)
        a = a - factor * pivot_row
    diagonal = jnp.sum(jnp.where(lanes == rows, a, 0.0), axis=1, keepdims=True)
    a = a / jnp.sqrt(diagonal)
    upper_ref[...] = jnp.where(lanes >= rows, a, 0.0)

    for i in range(n):
        total = jnp.broadcast_to(a[i : i + 1, n : n + 1], cols_ref.shape[1:]) * cols_ref[0]
        for j in range(1, i + 1):
            total = total + jnp.broadcast_to(a[i : i + 1, n + j : n + j + 1], cols_ref.shape[1:]) * cols_ref[j]
        result[i] = total

    fourth = peers(n, me, "vec", lambda to: result.at[to], back.at[me], s4, r4)
    for copy in fourth:
        copy.start()
    back[me] = result[me]
    for copy in fourth:
        copy.wait_recv()
    for copy in first + second + third + fourth:
        copy.wait_send()


def body(n, ns, perturbation, trajectory, step_order):
    pert, traj = perturbation[0], trajectory[0]
    fields, rows, cols = pert.shape
    count = fields * (rows // 8) * (cols // 128)
    per = -(-count // n)
    sections = traj.shape[0]
    chunks, bf = STEPS * sections * 3, traj.dtype
    vmem = pl.BlockSpec(memory_space=pltpu.VMEM)
    piece = pltpu.VMEM((chunks, rows, cols), bf)
    rim = pltpu.VMEM((STEPS * sections, fields, HALO, cols), bf)
    fringe = pltpu.VMEM((fields, HALO, cols), F32)
    full = pltpu.VMEM((fields, rows + 2 * HALO, cols), F32)
    slices = pltpu.VMEM((n, per * 8, 128), F32)
    small = pltpu.VMEM((n, 128), F32)
    dma = pltpu.SemaphoreType.DMA
    back, upper = pl.pallas_call(
        functools.partial(whole_kernel, n, ns, per, float(fields * rows * cols * ns)),
        out_shape=(
            jax.ShapeDtypeStruct((n, per * 8, 128), F32),
            jax.ShapeDtypeStruct((n, 128), F32),
        ),
        in_specs=[pl.BlockSpec(memory_space=pltpu.SMEM), vmem, vmem],
        out_specs=(vmem, vmem),
        scratch_shapes=[
            pltpu.VMEM((STEPS * sections, fields, rows, cols), bf),
            rim, rim, fringe, fringe,
            pltpu.VMEM((sections * 3, rows, cols), bf),
            piece, piece, piece, piece,
            pltpu.VMEM((STEPS * sections, 2, fields, HALO, cols), bf),
            full, full,
            slices, slices, slices,
            pltpu.VMEM((ns, n, 128), F32), pltpu.VMEM((n, n, 128), F32), small, small,
            dma((sections * 3,)), dma((sections * 3,)),
            dma((chunks,)), dma((chunks,)),
            dma((chunks,)), dma((chunks,)),
            dma((chunks,)), dma((chunks,)),
            dma((STEPS * sections, 2)), dma((STEPS * sections, 2)),
            dma((2,)), dma((2,)),
            dma((n,)), dma((n,)), dma((ns,)), dma((ns,)),
            dma((n,)), dma((n,)), dma((n,)), dma((n,)),
        ],
        compiler_params=pltpu.CompilerParams(collective_id=0, has_side_effects=True),
        name="whole",
    )(step_order, traj, pert)
    def finish(back_ref, upper_ref, out_ref, factor_ref):
        for number, (f, r, l) in enumerate(tiles_of(fields, rows, cols)):
            out_ref[f, r : r + 8, l : l + 128] = back_ref[number // per, pl.ds((number % per) * 8, 8), :]
        factor_ref[...] = upper_ref[:, :n]

    out, factor = pl.pallas_call(
        finish,
        out_shape=(jax.ShapeDtypeStruct(pert.shape, F32), jax.ShapeDtypeStruct((n, n), F32)),
        in_specs=[vmem, vmem],
        out_specs=(vmem, vmem),
        name="finish",
    )(back, upper)
    return out[None], factor


def solution(mesh):
    n, ns = mesh.shape["vec"], mesh.shape["space"]
    in_specs = (P("vec", None, "space", None), P("vec", None, None, "space", None), P())
    out_specs = (P("vec", None, "space", None), P())
    return jax.shard_map(
        functools.partial(body, n, ns), mesh=mesh, in_specs=in_specs, out_specs=out_specs, check_vma=False
    )
```

```python
import functools

import jax
import jax.numpy as jnp
from jax import lax
from jax.experimental import pallas as pl
from jax.experimental.pallas import tpu as pltpu
from jax.sharding import PartitionSpec as P

STEPS = 2
SECTIONS = 3
RIM_LAG = 10
LAG = 6
HALO = 8

GRAVITY_TOP = 1.0
GRAVITY_LOW = 0.5
DEPTH_TOP = 1.0
DEPTH_LOW = 1.0
CORIOLIS = 0.3
TIME_STEP = 0.25

MESH = pl.DeviceIdType.MESH
F32 = jnp.float32


def remote(src, dst, send, recv, target):
    return pltpu.make_async_remote_copy(
        src_ref=src, dst_ref=dst, send_sem=send, recv_sem=recv, device_id=target, device_id_type=MESH
    )


def diff_x(field):
    count = field.shape[0]
    return 0.5 * (pltpu.roll(field, count - 1, 0) - pltpu.roll(field, 1, 0))


def diff_y(field):
    count = field.shape[1]
    return 0.5 * (pltpu.roll(field, count - 1, 1) - pltpu.roll(field, 1, 1))


def tangent(base, state):
    dp_top = GRAVITY_TOP * (state[0] + state[3])
    dp_low = dp_top + GRAVITY_LOW * state[3]
    rates = []
    for layer, (mean_depth, pressure) in enumerate(((DEPTH_TOP, dp_top), (DEPTH_LOW, dp_low))):
        at = 3 * layer
        depth = base[at] + mean_depth
        u, v = base[at + 1], base[at + 2]
        dh, du, dv = state[at], state[at + 1], state[at + 2]
        rates.append(-diff_x(depth * du + dh * u) - diff_y(depth * dv + dh * v))
        rates.append(
            -(u * diff_x(du) + du * diff_x(u)) - (v * diff_y(du) + dv * diff_y(u))
            + CORIOLIS * dv - diff_x(pressure)
        )
        rates.append(
            -(u * diff_x(dv) + du * diff_x(v)) - (v * diff_y(dv) + dv * diff_y(v))
            - CORIOLIS * du - diff_y(pressure)
        )
    return rates


def tiles_of(fields, rows, cols):
    return [
        (f, r, l) for f in range(fields) for r in range(0, rows, 8) for l in range(0, cols, 128)
    ]


def whole_kernel(
    n, ns, direct, per, entries, order_ref, traj_ref, pert_ref,
    back, upper_ref,
    main, lo, hi, plo, phi, pair, in_up, in_dn, out_up, out_dn, edges, anchor, work,
    x_ref, cols_ref, result, gspace, gvec, mine_s, mine_v,
    sa, ra, su, ru, sd, rd, sc, rc, sh, rh, sp, rp,
    s1, r1, s2, r2, s3, r3, s4, r4,
):
    me = lax.axis_index("vec")
    tile = lax.axis_index("space")
    side = lax.rem(me, 2)
    line = me // 2
    lines = n // 2
    partner = me + 1 - 2 * side
    up_ok = line < lines - 1
    dn_ok = line > 0
    next_tile = lax.rem(tile + 1, ns)
    prev_tile = lax.rem(tile + ns - 1, ns)
    fields, rows, cols = pert_ref.shape
    chunks = STEPS * SECTIONS * 3
    parts = SECTIONS * 3

    barrier = pltpu.get_barrier_semaphore()
    pl.semaphore_signal(barrier, inc=1, device_id={"vec": partner}, device_id_type=MESH)
    near_tiles = (1, ns - 1) if ns <= 4 else range(1, ns)
    for d in near_tiles:
        pl.semaphore_signal(barrier, inc=1, device_id={"space": lax.rem(tile + d, ns)}, device_id_type=MESH)

    @pl.when(up_ok)
    def _():
        pl.semaphore_signal(barrier, inc=1, device_id={"vec": me + 2}, device_id_type=MESH)

    @pl.when(dn_ok)
    def _():
        pl.semaphore_signal(barrier, inc=1, device_id={"vec": me - 2}, device_id_type=MESH)

    pl.semaphore_wait(barrier, 1 + len(near_tiles) + up_ok.astype(jnp.int32) + dn_ok.astype(jnp.int32))

    def swap(p):
        k, f = lax.div(p, 3), lax.rem(p, 3)
        return remote(
            traj_ref.at[k, 3 * (1 - side) + f], pair.at[p], sa.at[p], ra.at[p], {"vec": partner}
        )

    def go_up(c):
        return remote(out_up.at[c], in_up.at[c], su.at[c], ru.at[c], {"vec": me + 2})

    def go_dn(c):
        return remote(out_dn.at[c], in_dn.at[c], sd.at[c], rd.at[c], {"vec": me - 2})

    def give(c):
        place = main.at[lax.div(c, 3), 3 * side + lax.rem(c, 3)]
        return remote(place, place, sc.at[c], rc.at[c], {"vec": partner})

    def edge_next(c):
        return remote(edges.at[c, 1], lo.at[c], sh.at[c, 1], rh.at[c, 1], {"space": next_tile})

    def edge_prev(c):
        return remote(edges.at[c, 0], hi.at[c], sh.at[c, 0], rh.at[c, 0], {"space": prev_tile})

    pert_next = remote(pert_ref.at[:, pl.ds(rows - HALO, HALO)], plo, sp.at[0], rp.at[0], {"space": next_tile})
    pert_prev = remote(pert_ref.at[:, pl.ds(0, HALO)], phi, sp.at[1], rp.at[1], {"space": prev_tile})

    @pl.loop(0, parts)
    def _(p):
        swap(p).start()

    pert_next.start()
    pert_prev.start()

    def owner_of(c):
        return jnp.where(c >= parts, order_ref[1], order_ref[0])

    def candidate(c):
        p = lax.rem(c, parts)
        own = traj_ref[lax.div(p, 3), 3 * side + lax.rem(p, 3)]
        return jnp.where(owner_of(c) == me, own, pair[p])

    def inside(c):
        return (c >= 0) & (c < chunks)

    near = LAG * jnp.minimum(line, lines - 1 - line)
    far = LAG * jnp.maximum(line, lines - 1 - line)
    anchor[:, HALO : HALO + rows] = pert_ref[...]

    @pl.loop(0, LAG * (lines - 1) + chunks + LAG + RIM_LAG)
    def _(t):
        c_pair = t - near
        c_up = t - LAG * line
        c_dn = t - LAG * (lines - 1 - line)
        c_fin = t - far
        c_edge = c_fin - LAG
        c_run = c_edge - RIM_LAG

        @pl.when((c_pair >= 0) & (c_pair < parts))
        def _():
            swap(c_pair).wait_recv()

        @pl.when(inside(c_up))
        def _():
            @pl.when(dn_ok)
            def _():
                go_up(c_up).wait_recv()

            @pl.when(up_ok)
            def _():
                here = lax.div(owner_of(c_up), 2) == line
                out_up[c_up] = jnp.where(here, candidate(c_up), in_up[c_up])
                go_up(c_up).start()

        @pl.when(inside(c_dn))
        def _():
            @pl.when(up_ok)
            def _():
                go_dn(c_dn).wait_recv()

            @pl.when(dn_ok)
            def _():
                here = lax.div(owner_of(c_dn), 2) == line
                out_dn[c_dn] = jnp.where(here, candidate(c_dn), in_dn[c_dn])
                go_dn(c_dn).start()

        @pl.when(inside(c_fin))
        def _():
            at = lax.div(owner_of(c_fin), 2)
            main[lax.div(c_fin, 3), 3 * side + lax.rem(c_fin, 3)] = jnp.where(
                at == line, candidate(c_fin), jnp.where(at < line, in_up[c_fin], in_dn[c_fin])
            )
            give(c_fin).start()

        @pl.when(inside(c_edge))
        def _():
            give(c_edge).wait_recv()

        @pl.when(inside(c_edge) & (lax.rem(c_edge, 3) == 2))
        def _():
            section = lax.div(c_edge, 3)
            edges[section, 0] = main[section, :, :HALO, :]
            edges[section, 1] = main[section, :, rows - HALO :, :]
            edge_next(section).start()
            edge_prev(section).start()

        @pl.when(c_run == 0)
        def _():
            pert_next.wait()
            pert_prev.wait()
            anchor[:, :HALO] = plo[...]
            anchor[:, HALO + rows :] = phi[...]
            work[...] = anchor[...]

        @pl.when(inside(c_run) & (lax.rem(c_run, 3) == 2))
        def _():
            number = lax.div(c_run, 3)
            section = lax.rem(number, SECTIONS)
            edge_next(number).wait()
            edge_prev(number).wait()
            base = [
                jnp.concatenate(
                    [
                        lo[number, f].astype(F32),
                        main[number, f].astype(F32),
                        hi[number, f].astype(F32),
                    ],
                    axis=0,
                )
                for f in range(fields)
            ]
            current = [work[f] for f in range(fields)]
            change = tangent(base, current)
            keep = jnp.where(section == 0, 0.0, jnp.where(section == 1, 0.75, 1.0 / 3.0)).astype(F32)
            take = jnp.where(section == 0, 1.0, jnp.where(section == 1, 0.25, 2.0 / 3.0)).astype(F32)
            for f in range(fields):
                work[f] = keep * anchor[f] + take * (current[f] + TIME_STEP * change[f])

            @pl.when(section == SECTIONS - 1)
            def _():
                anchor[...] = work[...]

    units = tiles_of(fields, rows, cols)
    for number, (f, r, l) in enumerate(units):
        x_ref[number // per, pl.ds((number % per) * 8, 8), :] = work[
            f, HALO + r : HALO + r + 8, l : l + 128
        ]
    for number in range(len(units), n * per):
        x_ref[number // per, pl.ds((number % per) * 8, 8), :] = jnp.zeros((8, 128), F32)

    def peers(count, here, axis, src, dst, send, recv):
        made = []
        for d in range(1, count):
            to = lax.rem(here + d, count)
            made.append(remote(src(to), dst, send.at[d], recv.at[d], {axis: to}))
        return made

    first = peers(n, me, "vec", lambda to: x_ref.at[to], cols_ref.at[me], s1, r1)
    for copy in first:
        copy.start()
    cols_ref[me] = x_ref[me]

    @pl.loop(0, parts)
    def _(p):
        swap(p).wait_send()

    @pl.loop(0, chunks)
    def _(c):
        give(c).wait_send()

        @pl.when(up_ok)
        def _():
            go_up(c).wait_send()

        @pl.when(dn_ok)
        def _():
            go_dn(c).wait_send()

    for copy in first:
        copy.wait_recv()

    lanes = lax.broadcasted_iota(jnp.int32, (n, 128), 1)
    rows = lax.broadcasted_iota(jnp.int32, (n, 128), 0)
    gram = jnp.zeros((n, 128), F32)
    for i in range(n):
        line = jnp.sum(cols_ref[...] * cols_ref[i][None], axis=1)
        gram = gram + jnp.where(lanes == i, jnp.sum(line, axis=1, keepdims=True), 0.0)

    everyone = []
    if direct:
        mine_s[...] = gram
        for e in range(1, n * ns):
            dv, ds = e // ns, e % ns
            place = gvec.at[me * ns + tile]
            where = {"vec": lax.rem(me + dv, n), "space": lax.rem(tile + ds, ns)}
            everyone.append(remote(mine_s, place, s3.at[e], r3.at[e], where))
        everyone.reverse()
        for copy in everyone:
            copy.start()
        gvec[me * ns + tile] = gram
        for copy in everyone:
            copy.wait_recv()
        gram = gvec[0]
        for i in range(1, n * ns):
            gram = gram + gvec[i]
    else:
        mine_s[...] = gram
        second = peers(ns, tile, "space", lambda to: mine_s, gspace.at[tile], s2, r2)
        everyone += second
        for copy in second:
            copy.start()
        gspace[tile] = gram
        for copy in second:
            copy.wait_recv()
        gram = gspace[0]
        for i in range(1, ns):
            gram = gram + gspace[i]

        mine_v[...] = gram
        third = peers(n, me, "vec", lambda to: mine_v, gvec.at[me], s3, r3)
        everyone += third
        for copy in third:
            copy.start()
        gvec[me] = gram
        for copy in third:
            copy.wait_recv()
        gram = gvec[0]
        for i in range(1, n):
            gram = gram + gvec[i]

    a = jnp.where(lanes < n, gram / entries, 0.0) + jnp.where(lanes == rows + n, 1.0, 0.0)
    for k in range(n):
        pivot_row = a[k : k + 1, :]
        column = jnp.sum(jnp.where(lanes == k, a, 0.0), axis=1, keepdims=True)
        factor = jnp.where(rows[:, :1] > k, column / column[k : k + 1, :], 0.0)
        a = a - factor * pivot_row
    diagonal = jnp.sum(jnp.where(lanes == rows, a, 0.0), axis=1, keepdims=True)
    a = a / jnp.sqrt(diagonal)
    upper_ref[...] = jnp.where(lanes >= rows, a, 0.0)

    for i in range(n):
        total = jnp.broadcast_to(a[i : i + 1, n : n + 1], cols_ref.shape[1:]) * cols_ref[0]
        for j in range(1, i + 1):
            total = total + jnp.broadcast_to(a[i : i + 1, n + j : n + j + 1], cols_ref.shape[1:]) * cols_ref[j]
        result[i] = total

    fourth = peers(n, me, "vec", lambda to: result.at[to], back.at[me], s4, r4)
    for copy in fourth:
        copy.start()
    back[me] = result[me]
    for copy in fourth:
        copy.wait_recv()
    for copy in first + everyone + fourth:
        copy.wait_send()


def body(n, ns, perturbation, trajectory, step_order):
    pert, traj = perturbation[0], trajectory[0]
    fields, rows, cols = pert.shape
    count = fields * (rows // 8) * (cols // 128)
    per = -(-count // n)
    sections = traj.shape[0]
    direct = n * ns <= 64
    slots = n * ns if direct else n
    chunks, bf = STEPS * sections * 3, traj.dtype
    vmem = pl.BlockSpec(memory_space=pltpu.VMEM)
    piece = pltpu.VMEM((chunks, rows, cols), bf)
    rim = pltpu.VMEM((STEPS * sections, fields, HALO, cols), bf)
    fringe = pltpu.VMEM((fields, HALO, cols), F32)
    full = pltpu.VMEM((fields, rows + 2 * HALO, cols), F32)
    slices = pltpu.VMEM((n, per * 8, 128), F32)
    small = pltpu.VMEM((n, 128), F32)
    dma = pltpu.SemaphoreType.DMA
    back, upper = pl.pallas_call(
        functools.partial(whole_kernel, n, ns, direct, per, float(fields * rows * cols * ns)),
        out_shape=(
            jax.ShapeDtypeStruct((n, per * 8, 128), F32),
            jax.ShapeDtypeStruct((n, 128), F32),
        ),
        in_specs=[pl.BlockSpec(memory_space=pltpu.SMEM), vmem, vmem],
        out_specs=(vmem, vmem),
        scratch_shapes=[
            pltpu.VMEM((STEPS * sections, fields, rows, cols), bf),
            rim, rim, fringe, fringe,
            pltpu.VMEM((sections * 3, rows, cols), bf),
            piece, piece, piece, piece,
            pltpu.VMEM((STEPS * sections, 2, fields, HALO, cols), bf),
            full, full,
            slices, slices, slices,
            pltpu.VMEM((ns, n, 128), F32), pltpu.VMEM((slots, n, 128), F32), small, small,
            dma((sections * 3,)), dma((sections * 3,)),
            dma((chunks,)), dma((chunks,)),
            dma((chunks,)), dma((chunks,)),
            dma((chunks,)), dma((chunks,)),
            dma((STEPS * sections, 2)), dma((STEPS * sections, 2)),
            dma((2,)), dma((2,)),
            dma((n,)), dma((n,)), dma((ns,)), dma((ns,)),
            dma((slots,)), dma((slots,)), dma((n,)), dma((n,)),
        ],
        compiler_params=pltpu.CompilerParams(collective_id=0, has_side_effects=True),
        name="whole",
    )(step_order, traj, pert)
    def finish(back_ref, upper_ref, out_ref, factor_ref):
        for number, (f, r, l) in enumerate(tiles_of(fields, rows, cols)):
            out_ref[f, r : r + 8, l : l + 128] = back_ref[number // per, pl.ds((number % per) * 8, 8), :]
        factor_ref[...] = upper_ref[:, :n]

    out, factor = pl.pallas_call(
        finish,
        out_shape=(jax.ShapeDtypeStruct(pert.shape, F32), jax.ShapeDtypeStruct((n, n), F32)),
        in_specs=[vmem, vmem],
        out_specs=(vmem, vmem),
        name="finish",
    )(back, upper)
    return out[None], factor


def solution(mesh):
    n, ns = mesh.shape["vec"], mesh.shape["space"]
    in_specs = (P("vec", None, "space", None), P("vec", None, None, "space", None), P())
    out_specs = (P("vec", None, "space", None), P())
    return jax.shard_map(
        functools.partial(body, n, ns), mesh=mesh, in_specs=in_specs, out_specs=out_specs, check_vma=False
    )
```
